32 devices in a mesh: pts: 16 (over z, x, core), modes: 2 (over y).
Axes of the slice: x: 2, y: 2, z: 4, core: 2. Of those that a mesh axis runs over, the one named last changes fastest.
Arguments:
- features: bfloat16 [65536, 128], P('pts'), may hold values from -6 to 6
- coords: float32 [3, 65536], P(None, 'pts'), may hold values from 0 to 1
- quad_weight: float32 [65536], P('pts'), may hold values from 0.5 to 6, as said below
- mode_table: int32 [3, 8192], replicated, may hold values from -8 to 31, as said below
- mode_weight: bfloat16 [8192, 2, 128, 128], P(('pts', 'modes')), may hold values from -4 to 4
- lin_weight: bfloat16 [128, 128], replicated, may hold values from -0.5 to 0.5
- bias: float32 [128], replicated, may hold values from -3 to 3
Outputs:
- output: bfloat16 [65536, 128], P(('pts', 'modes'))
The draws below stay inside these ranges and needn't reach their ends.
Inputs may be any that keep to these rules, and one draw needn't show every extreme that they name: `mode_table`: each column is a distinct triple (kx, ky, kz) with -8 <= kx < 8, -8 <= ky < 8, 0 <= kz < 32; every such triple appears exactly once, in an order drawn from the seed. `quad_weight`: Positive.
All inputs are finite; a program needn't handle non-finite values.
Results may differ from the reference program's by a relative error of at most 0.018.
Values may be sent and summed in bfloat16 or wider, within the bound.
A program may use at most 128 MiB of HBM per device.

```python
import math
import jax
import jax.numpy as jnp
from jax import lax

C = 128
MX = 16
MY = 16
MZ = 32
MODES = 8192
TOTAL = 65536


def draw_quad_weight(key, part):
    ramp = 1.0 + 2.0 * jnp.arange(TOTAL, dtype=jnp.float32) / (TOTAL - 1)
    base = jnp.exp(jax.random.uniform(key, (TOTAL,), jnp.float32, jnp.log(0.5), jnp.log(2.0)))
    return jnp.clip(base * ramp, 0.5, 6.0).astype(jnp.float32)


def draw_mode_table(key, part):
    order = jax.random.permutation(jax.random.fold_in(key, 7), MODES).astype(jnp.int32)
    kx_num = order // (MY * MZ) - MX // 2
    ky_num = order // MZ % MY - MY // 2
    kz_num = order % MZ
    return jnp.stack([kx_num, ky_num, kz_num]).astype(jnp.int32)


def block_scale(stream_key, extent, pieces, low, top_value):
    level, own = 1.0, jax.random.fold_in(stream_key, 6)
    for dim, blocks in pieces:
        draws = jnp.exp(jax.random.uniform(jax.random.fold_in(own, dim), (blocks,), jnp.float32, low / len(pieces), top_value / len(pieces)))
        level = level * jnp.repeat(draws, extent[dim] // blocks).reshape([-1 if axis == dim else 1 for axis in range(len(extent))])
    return level


def gaussian(rng, extent, scale, limit, shards=(), kind=jnp.bfloat16):
    values = scale * jax.random.normal(rng, extent, jnp.float32)
    if shards:
        values = values * block_scale(rng, extent, shards, -0.22, 0.18)
    return jnp.clip(values, -limit, limit).astype(kind)


def setup_inputs(seed: int = 0) -> dict:
    streams_of = jax.random.split(jax.random.key(seed), 8)
    features = gaussian(streams_of[0], (TOTAL, C), 1.0, 6.0, ((0, 16),))
    coords = jnp.clip(1.0 * jax.random.uniform(streams_of[1], (3, TOTAL), jnp.float32) ** block_scale(streams_of[1], (3, TOTAL), ((1, 16),), -0.2, 0.2), 0.0, 1.0)
    quad_weight = draw_quad_weight(jax.random.fold_in(streams_of[7], 71), 0)
    mode_table = draw_mode_table(jax.random.fold_in(streams_of[7], 71), 0)
    mode_weight = gaussian(streams_of[4], (MODES, 2, C, C), ((TOTAL / (MODES * C)) ** 0.5), 4.0, ((0, 32),))
    lin_weight = gaussian(streams_of[5], (C, C), C ** -0.5, 0.5)
    bias = gaussian(streams_of[6], (C,), 0.5, 3.0, (), jnp.float32)
    return {"features": features, "coords": coords, "quad_weight": quad_weight, "mode_table": mode_table, "mode_weight": mode_weight, "lin_weight": lin_weight, "bias": bias}


def phase_basis(coords, wave):
    turns = coords[0][:, None] * wave[0][None, :] + coords[1][:, None] * wave[1][None, :]
    turns = turns + coords[2][:, None] * wave[2][None, :]
    angle = (2.0 * math.pi) * turns
    return jnp.concatenate([jnp.cos(angle), -jnp.sin(angle)], axis=1).astype(jnp.bfloat16)


def reference(features, coords, quad_weight, mode_table, mode_weight, lin_weight, bias):
    weighted = (quad_weight[:, None] * features.astype(jnp.float32)).astype(jnp.bfloat16)
    total = jnp.sum(quad_weight)
    wave = mode_table.astype(jnp.float32)
    blocks = MODES // 256
    wave_blocks = wave.reshape(3, blocks, 256).transpose(1, 0, 2)
    weighted_f = weighted.astype(jnp.float32)

    def analyse(part_wave):
        basis = phase_basis(coords, part_wave).astype(jnp.float32)
        res = lax.dot_general(basis, weighted_f, (((0,), (0,)), ((), ())), preferred_element_type=jnp.float32)
        return res.reshape(2, 256, C).transpose(1, 0, 2).reshape(256, 2 * C)

    coef = lax.map(analyse, wave_blocks).reshape(MODES, 2 * C).astype(jnp.bfloat16)
    real_in = coef[:, :C].astype(jnp.float32)
    imag_in = coef[:, C:].astype(jnp.float32)
    w_real = mode_weight[:, 0].astype(jnp.float32)
    w_imag = mode_weight[:, 1].astype(jnp.float32)
    real_out = jnp.einsum("mc,mcd->md", real_in, w_real) - jnp.einsum("mc,mcd->md", imag_in, w_imag)
    imag_out = jnp.einsum("mc,mcd->md", real_in, w_imag) + jnp.einsum("mc,mcd->md", imag_in, w_real)
    filtered = jnp.concatenate([real_out, imag_out], axis=1).astype(jnp.bfloat16)
    filt_blocks = filtered.reshape(blocks, 256, 2 * C)

    def synthesize(carry, inputs):
        part_wave, piece = inputs
        basis = phase_basis(coords, part_wave).astype(jnp.float32)
        rhs = jnp.concatenate([piece[:, :C], piece[:, C:]], axis=0).astype(jnp.float32)
        return carry + jnp.dot(basis, rhs, preferred_element_type=jnp.float32), None

    spectral, unused = lax.scan(synthesize, jnp.zeros((TOTAL, C), jnp.float32), (wave_blocks, filt_blocks))
    linear = jnp.dot(features, lin_weight, preferred_element_type=jnp.float32)
    pre = spectral / total + linear + bias[None, :]
    return jax.nn.gelu(pre, approximate=False).astype(jnp.bfloat16)
```

```python
import math

import jax
import jax.numpy as jnp
from jax import lax
from jax.sharding import PartitionSpec as P

KX_LOW, KX_COUNT = -8, 16
KY_LOW, KY_COUNT = -8, 16
KZ_LOW, KZ_COUNT = 0, 32
HALF = KX_COUNT // 2
PLANE = KY_COUNT * KZ_COUNT
AXES = ("pts", "modes")


def cos_sin(turns):
    angle = (2.0 * math.pi) * (turns - jnp.round(turns))
    return jnp.cos(angle), jnp.sin(angle)


def factors(coords):
    x, y, z = coords[0], coords[1], coords[2]
    j = jnp.arange(HALF, dtype=jnp.float32) + 0.5
    xc, xs = cos_sin(j[:, None] * x[None, :])
    ky = jnp.arange(KY_COUNT, dtype=jnp.float32) + KY_LOW
    kz = jnp.arange(KZ_COUNT, dtype=jnp.float32) + KZ_LOW
    yc, ys = cos_sin(ky[:, None] * y[None, :])
    zc, zs = cos_sin(kz[:, None] * z[None, :] - 0.5 * x[None, :])
    yc, ys = yc[:, None, :], ys[:, None, :]
    zc, zs = zc[None], zs[None]
    e_re = (yc * zc - ys * zs).reshape(PLANE, -1)
    e_im = (ys * zc + yc * zs).reshape(PLANE, -1)
    e = jnp.concatenate([e_re, e_im], axis=0).astype(jnp.bfloat16)
    return jnp.concatenate([xc, xs], axis=0), e


def grid_index(mode_table):
    kx = mode_table[0]
    slot = jnp.where(kx >= 0, kx, HALF - 1 - kx)
    return (slot * KY_COUNT + mode_table[1] - KY_LOW) * KZ_COUNT + mode_table[2] - KZ_LOW


def inverse_index(index):
    n = index.shape[0]
    lo = 128
    hi = n // lo
    ids = jnp.arange(n, dtype=jnp.int32)
    hot_lo = (index[:, None] % lo == jnp.arange(lo)[None, :]).astype(jnp.bfloat16)
    hit = index[None, :] // lo == jnp.arange(hi)[:, None]
    top = jnp.where(hit, ids[None, :] // lo, 0).astype(jnp.bfloat16)
    low = jnp.where(hit, ids[None, :] % lo, 0).astype(jnp.bfloat16)
    got = jnp.dot(jnp.concatenate([top, low], axis=0), hot_lo, preferred_element_type=jnp.float32)
    return (got[:hi] * lo + got[hi:]).astype(jnp.int32).reshape(n)


def on_device(features, coords, quad_weight, mode_table, mode_weight, lin_weight, bias):
    width = features.shape[1]
    n_groups = lax.axis_size("modes")
    group = lax.axis_index("modes")
    rows = features.shape[0] // n_groups
    total = lax.psum(jnp.sum(quad_weight), "pts")
    features = lax.dynamic_slice_in_dim(features, group * rows, rows, 0)
    coords = lax.dynamic_slice_in_dim(coords, group * rows, rows, 1)
    quad = lax.dynamic_slice_in_dim(quad_weight, group * rows, rows, 0)
    xf, e = factors(coords)
    index = grid_index(mode_table)
    inverse = inverse_index(index)
    weighted = (quad[:, None] * features.astype(jnp.float32)).astype(jnp.bfloat16)
    xw = (xf.T[:, :, None] * weighted.astype(jnp.float32)[:, None, :]).astype(jnp.bfloat16)
    term = jnp.dot(e, xw.reshape(rows, KX_COUNT * width), preferred_element_type=jnp.float32)
    term = term.reshape(2, PLANE, 2, HALF, width)
    a, b, c, d = term[0, :, 0], term[1, :, 1], term[1, :, 0], term[0, :, 1]
    pos = jnp.concatenate([a - b, -(c + d)], axis=-1)
    neg = jnp.concatenate([a + b, d - c], axis=-1)
    coef = jnp.concatenate([pos, neg], axis=1).astype(jnp.bfloat16)
    coef = coef.transpose(1, 0, 2).reshape(KX_COUNT * PLANE, 2 * width)
    coef = jnp.take(coef, index, axis=0, mode="clip")
    coef = lax.psum_scatter(coef, AXES, scatter_dimension=0, tiled=True)
    real_in = coef[:, :width]
    imag_in = coef[:, width:]
    w_real = mode_weight[:, 0]
    w_imag = mode_weight[:, 1]
    real_out = jnp.einsum(
        "mc,mcd->md", real_in, w_real, preferred_element_type=jnp.float32
    ) - jnp.einsum("mc,mcd->md", imag_in, w_imag, preferred_element_type=jnp.float32)
    imag_out = jnp.einsum(
        "mc,mcd->md", real_in, w_imag, preferred_element_type=jnp.float32
    ) + jnp.einsum("mc,mcd->md", imag_in, w_real, preferred_element_type=jnp.float32)
    filtered = jnp.concatenate([real_out, imag_out], axis=1).astype(jnp.bfloat16)
    full = lax.all_gather(filtered, AXES, axis=0, tiled=True)
    full = jnp.take(full, inverse, axis=0, mode="clip").astype(jnp.float32)
    full = full.reshape(2, HALF, PLANE, 2, width)
    pos_re, pos_im = full[0, :, :, 0], full[0, :, :, 1]
    neg_re, neg_im = full[1, :, :, 0], full[1, :, :, 1]
    by_re = jnp.concatenate([pos_re + neg_re, neg_im - pos_im], axis=0)
    by_im = jnp.concatenate([-(pos_im + neg_im), neg_re - pos_re], axis=0)
    rhs = jnp.concatenate([by_re, by_im], axis=1).astype(jnp.bfloat16)
    rhs = rhs.transpose(1, 0, 2).reshape(2 * PLANE, KX_COUNT * width)
    field = lax.dot_general(e, rhs, (((0,), (0,)), ((), ())), preferred_element_type=jnp.float32)
    field = field.reshape(rows, KX_COUNT, width) * xf.T[:, :, None]
    spectral = jnp.sum(field, axis=1)
    linear = jnp.dot(features, lin_weight, preferred_element_type=jnp.float32)
    pre = spectral / total + linear + bias[None, :]
    return jax.nn.gelu(pre, approximate=False).astype(jnp.bfloat16)


def solution(mesh):
    return jax.shard_map(
        on_device,
        mesh=mesh,
        in_specs=(
            P("pts", None),
            P(None, "pts"),
            P("pts"),
            P(),
            P(("pts", "modes"), None, None, None),
            P(),
            P(),
        ),
        out_specs=P(("pts", "modes"), None),
        check_vma=False,
    )
```

```python
import math

import jax
import jax.numpy as jnp
from jax import lax
from jax.experimental import pallas as pl
from jax.experimental.pallas import tpu as pltpu
from jax.sharding import PartitionSpec as P

KX_LOW, KX_COUNT = -8, 16
KY_LOW, KY_COUNT = -8, 16
KZ_LOW, KZ_COUNT = 0, 32
HALF = KX_COUNT // 2
PLANE = KY_COUNT * KZ_COUNT
AXES = ("pts", "modes")
TAIL = 16


def cos_sin(turns):
    angle = (2.0 * math.pi) * (turns - jnp.round(turns))
    return jnp.cos(angle), jnp.sin(angle)


def factors(coords):
    x, y, z = coords[0], coords[1], coords[2]
    j = jnp.arange(HALF, dtype=jnp.float32) + 0.5
    xc, xs = cos_sin(j[:, None] * x[None, :])
    ky = jnp.arange(KY_COUNT, dtype=jnp.float32) + KY_LOW
    kz = jnp.arange(KZ_COUNT, dtype=jnp.float32) + KZ_LOW
    yc, ys = cos_sin(ky[:, None] * y[None, :])
    zc, zs = cos_sin(kz[:, None] * z[None, :] - 0.5 * x[None, :])
    return jnp.concatenate([xc, xs], axis=0).T, (yc, ys, zc, zs)


def plane_kernel(yc_ref, ys_ref, zc_ref, zs_ref, e_ref, et_ref):
    zc, zs = zc_ref[...], zs_ref[...]
    for k in range(KY_COUNT):
        yc, ys = yc_ref[pl.ds(k, 1)], ys_ref[pl.ds(k, 1)]
        re = yc * zc - ys * zs
        im = ys * zc + yc * zs
        e_ref[pl.ds(k * KZ_COUNT, KZ_COUNT)] = re.astype(jnp.bfloat16)
        e_ref[pl.ds(PLANE + k * KZ_COUNT, KZ_COUNT)] = im.astype(jnp.bfloat16)
    et_ref[...] = e_ref[...].T


def plane_factors(parts):
    rows = parts[0].shape[1]
    step = math.gcd(rows, 512)
    return pl.pallas_call(
        plane_kernel,
        grid=(rows // step,),
        out_shape=(
            jax.ShapeDtypeStruct((2 * PLANE, rows), jnp.bfloat16),
            jax.ShapeDtypeStruct((rows, 2 * PLANE), jnp.bfloat16),
        ),
        in_specs=[pl.BlockSpec((part.shape[0], step), lambda p: (0, p)) for part in parts],
        out_specs=(
            pl.BlockSpec((2 * PLANE, step), lambda p: (0, p)),
            pl.BlockSpec((step, 2 * PLANE), lambda p: (p, 0)),
        ),
        compiler_params=pltpu.CompilerParams(vmem_limit_bytes=48 << 20),
    )(*parts)


def column(table_ref, at):
    lanes = lax.broadcasted_iota(jnp.int32, table_ref.shape, 1)
    return jnp.sum(jnp.where(lanes == at, table_ref[...], 0.0), axis=1, keepdims=True)


def analyse_kernel(e_ref, xf_ref, weighted_ref, out_ref):
    j = pl.program_id(0)
    width = weighted_ref.shape[1]
    weighted = weighted_ref[...].astype(jnp.float32)
    by_cos = (column(xf_ref, j) * weighted).astype(jnp.bfloat16)
    by_sin = (column(xf_ref, HALF + j) * weighted).astype(jnp.bfloat16)
    rhs = jnp.concatenate([by_cos, by_sin], axis=1)
    re = jnp.dot(e_ref[:PLANE], rhs, preferred_element_type=jnp.float32)
    im = jnp.dot(e_ref[PLANE:], rhs, preferred_element_type=jnp.float32)
    rc, rs = re[:, :width], re[:, width:]
    ic, is_ = im[:, :width], im[:, width:]
    out_ref[0, 0, :, :width] = (rc - is_).astype(jnp.bfloat16)
    out_ref[0, 0, :, width:] = (-(ic + rs)).astype(jnp.bfloat16)
    out_ref[1, 0, :, :width] = (rc + is_).astype(jnp.bfloat16)
    out_ref[1, 0, :, width:] = (rs - ic).astype(jnp.bfloat16)


def analyse(e, xf, weighted):
    rows, width = weighted.shape
    out = pl.pallas_call(
        analyse_kernel,
        grid=(HALF,),
        out_shape=jax.ShapeDtypeStruct((2, HALF, PLANE, 2 * width), jnp.bfloat16),
        in_specs=[
            pl.BlockSpec((2 * PLANE, rows), lambda j: (0, 0)),
            pl.BlockSpec((rows, 2 * HALF), lambda j: (0, 0)),
            pl.BlockSpec((rows, width), lambda j: (0, 0)),
        ],
        out_specs=pl.BlockSpec((2, 1, PLANE, 2 * width), lambda j: (0, j, 0, 0)),
        compiler_params=pltpu.CompilerParams(vmem_limit_bytes=48 << 20),
    )(e, xf, weighted)
    return out.reshape(2 * HALF * PLANE, 2 * width)


def synthesize_kernel(et_ref, xf_ref, full_ref, out_ref):
    j = pl.program_id(0)
    width = out_ref.shape[1]
    pos = full_ref[0, 0].astype(jnp.float32)
    neg = full_ref[1, 0].astype(jnp.float32)
    pr, pi = pos[:, :width], pos[:, width:]
    nr, ni = neg[:, :width], neg[:, width:]
    top = jnp.concatenate([pr + nr, ni - pi], axis=1).astype(jnp.bfloat16)
    low = jnp.concatenate([-(pi + ni), nr - pr], axis=1).astype(jnp.bfloat16)
    field = jnp.dot(et_ref[:, :PLANE], top, preferred_element_type=jnp.float32)
    field = field + jnp.dot(et_ref[:, PLANE:], low, preferred_element_type=jnp.float32)
    add = column(xf_ref, j) * field[:, :width] + column(xf_ref, HALF + j) * field[:, width:]

    @pl.when(j == 0)
    def _():
        out_ref[...] = add

    @pl.when(j > 0)
    def _():
        out_ref[...] += add


def synthesize(et, xf, full):
    rows = et.shape[0]
    width = full.shape[1] // 2
    return pl.pallas_call(
        synthesize_kernel,
        grid=(HALF,),
        out_shape=jax.ShapeDtypeStruct((rows, width), jnp.float32),
        in_specs=[
            pl.BlockSpec((rows, 2 * PLANE), lambda j: (0, 0)),
            pl.BlockSpec((rows, 2 * HALF), lambda j: (0, 0)),
            pl.BlockSpec((2, 1, PLANE, 2 * width), lambda j: (0, j, 0, 0)),
        ],
        out_specs=pl.BlockSpec((rows, width), lambda j: (0, 0)),
        compiler_params=pltpu.CompilerParams(vmem_limit_bytes=48 << 20),
    )(et, xf, full.reshape(2, HALF, PLANE, 2 * width))


def filter_kernel(coef_ref, w_ref, out_ref):
    width = w_ref.shape[2]
    for m in range(w_ref.shape[0]):
        pair = coef_ref[m]
        by_re = jnp.dot(pair, w_ref[m, 0], preferred_element_type=jnp.float32)
        by_im = jnp.dot(pair, w_ref[m, 1], preferred_element_type=jnp.float32)
        out_ref[pl.ds(m, 1), :width] = by_re[0:1] - by_im[1:2]
        out_ref[pl.ds(m, 1), width:] = by_im[0:1] + by_re[1:2]


def filter_modes(coef, weight):
    modes, width = weight.shape[0], weight.shape[2]
    step = math.gcd(modes, 16)
    return pl.pallas_call(
        filter_kernel,
        grid=(modes // step,),
        out_shape=jax.ShapeDtypeStruct((modes, 2 * width), jnp.float32),
        in_specs=[
            pl.BlockSpec((step, 2, width), lambda m: (m, 0, 0)),
            pl.BlockSpec((step, 2, width, width), lambda m: (m, 0, 0, 0)),
        ],
        out_specs=pl.BlockSpec((step, 2 * width), lambda m: (m, 0)),
        compiler_params=pltpu.CompilerParams(vmem_limit_bytes=48 << 20),
    )(coef.reshape(modes, 2, width), weight)


def grid_index(mode_table):
    kx = mode_table[0]
    slot = jnp.where(kx >= 0, kx, HALF - 1 - kx)
    return (slot * KY_COUNT + mode_table[1] - KY_LOW) * KZ_COUNT + mode_table[2] - KZ_LOW


def inverse_index(index):
    n = index.shape[0]
    lo = 128
    hi = n // lo
    ids = jnp.arange(n, dtype=jnp.int32)
    hot_lo = (index[:, None] % lo == jnp.arange(lo)[None, :]).astype(jnp.bfloat16)
    hit = index[None, :] // lo == jnp.arange(hi)[:, None]
    top = jnp.where(hit, ids[None, :] // lo, 0).astype(jnp.bfloat16)
    low = jnp.where(hit, ids[None, :] % lo, 0).astype(jnp.bfloat16)
    got = jnp.dot(jnp.concatenate([top, low], axis=0), hot_lo, preferred_element_type=jnp.float32)
    return (got[:hi] * lo + got[hi:]).astype(jnp.int32).reshape(n)


def on_device(features, coords, quad_weight, mode_table, mode_weight, lin_weight, bias):
    width = features.shape[1]
    n_groups = lax.axis_size("modes")
    group = lax.axis_index("modes")
    rows = features.shape[0] // n_groups
    features = lax.dynamic_slice_in_dim(features, group * rows, rows, 0)
    coords = lax.dynamic_slice_in_dim(coords, group * rows, rows, 1)
    quad = lax.dynamic_slice_in_dim(quad_weight, group * rows, rows, 0)
    own = mode_weight.shape[0]
    xf, parts = factors(coords)
    e, et = plane_factors(parts)
    index = grid_index(mode_table)
    inverse = inverse_index(index)
    weighted = (quad[:, None] * features.astype(jnp.float32)).astype(jnp.bfloat16)
    coef = analyse(e, xf, weighted)
    coef = jnp.take(coef, index, axis=0, mode="clip")
    coef = lax.all_to_all(coef.reshape(-1, own, 2 * width), AXES, 0, 0)
    coef = jnp.sum(coef.astype(jnp.float32), axis=0).astype(jnp.bfloat16)
    filtered = filter_modes(coef, mode_weight).astype(jnp.bfloat16)
    share = jnp.sum(quad)
    high = lax.reduce_precision(share, 8, 7)
    mid = lax.reduce_precision(share - high, 8, 7)
    low = share - high - mid
    cells = jnp.pad(jnp.stack([high, mid, low]), (0, 2 * width - 3))
    cells = jnp.broadcast_to(cells[None], (TAIL, 2 * width)).astype(jnp.bfloat16)
    sent = jnp.concatenate([filtered, cells], axis=0)
    full = lax.all_gather(sent, AXES, axis=0, tiled=True)
    devices = full.shape[0] // (own + TAIL)
    shares = full.reshape(devices, own + TAIL, 2 * width)[:, own, :3]
    total = jnp.sum(shares.astype(jnp.float32))
    full = jnp.take(full, inverse + inverse // own * TAIL, axis=0, mode="clip")
    spectral = synthesize(et, xf, full)
    linear = jnp.dot(features, lin_weight, preferred_element_type=jnp.float32)
    pre = spectral / total + linear + bias[None, :]
    return jax.nn.gelu(pre, approximate=False).astype(jnp.bfloat16)


def solution(mesh):
    return jax.shard_map(
        on_device,
        mesh=mesh,
        in_specs=(
            P("pts", None),
            P(None, "pts"),
            P("pts"),
            P(),
            P(("pts", "modes"), None, None, None),
            P(),
            P(),
        ),
        out_specs=P(("pts", "modes"), None),
        check_vma=False,
    )
```

```python
import math

import jax
import jax.numpy as jnp
from jax import lax
from jax.experimental import pallas as pl
from jax.experimental.pallas import tpu as pltpu
from jax.sharding import Mesh
from jax.sharding import PartitionSpec as P

KX_LOW, KX_COUNT = -8, 16
KY_LOW, KY_COUNT = -8, 16
KZ_LOW, KZ_COUNT = 0, 32
HALF = KX_COUNT // 2
PLANE = KY_COUNT * KZ_COUNT
PTS = ("chip", "core")
AXES = PTS + ("modes",)
TAIL = 16


def cos_sin(turns):
    angle = (2.0 * math.pi) * (turns - jnp.round(turns))
    return jnp.cos(angle), jnp.sin(angle)


def factors(coords):
    x, y, z = coords[0], coords[1], coords[2]
    j = jnp.arange(HALF, dtype=jnp.float32) + 0.5
    xc, xs = cos_sin(j[:, None] * x[None, :])
    ky = jnp.arange(KY_COUNT, dtype=jnp.float32) + KY_LOW
    kz = jnp.arange(KZ_COUNT, dtype=jnp.float32) + KZ_LOW
    yc, ys = cos_sin(ky[:, None] * y[None, :])
    zc, zs = cos_sin(kz[:, None] * z[None, :] - 0.5 * x[None, :])
    return jnp.concatenate([xc, xs], axis=0).T, (yc, ys, zc, zs)


def plane_kernel(yc_ref, ys_ref, zc_ref, zs_ref, e_ref, et_ref):
    zc, zs = zc_ref[...], zs_ref[...]
    for k in range(KY_COUNT):
        yc, ys = yc_ref[pl.ds(k, 1)], ys_ref[pl.ds(k, 1)]
        re = yc * zc - ys * zs
        im = ys * zc + yc * zs
        e_ref[pl.ds(k * KZ_COUNT, KZ_COUNT)] = re.astype(jnp.bfloat16)
        e_ref[pl.ds(PLANE + k * KZ_COUNT, KZ_COUNT)] = im.astype(jnp.bfloat16)
    et_ref[...] = e_ref[...].T


def plane_factors(parts):
    rows = parts[0].shape[1]
    step = math.gcd(rows, 512)
    return pl.pallas_call(
        plane_kernel,
        grid=(rows // step,),
        out_shape=(
            jax.ShapeDtypeStruct((2 * PLANE, rows), jnp.bfloat16),
            jax.ShapeDtypeStruct((rows, 2 * PLANE), jnp.bfloat16),
        ),
        in_specs=[pl.BlockSpec((part.shape[0], step), lambda p: (0, p)) for part in parts],
        out_specs=(
            pl.BlockSpec((2 * PLANE, step), lambda p: (0, p)),
            pl.BlockSpec((step, 2 * PLANE), lambda p: (p, 0)),
        ),
        compiler_params=pltpu.CompilerParams(vmem_limit_bytes=48 << 20),
    )(*parts)


def column(table_ref, at):
    lanes = lax.broadcasted_iota(jnp.int32, table_ref.shape, 1)
    return jnp.sum(jnp.where(lanes == at, table_ref[...], 0.0), axis=1, keepdims=True)


def analyse_kernel(e_ref, xf_ref, weighted_ref, out_ref):
    j = pl.program_id(0)
    width = weighted_ref.shape[1]
    weighted = weighted_ref[...].astype(jnp.float32)
    by_cos = (column(xf_ref, j) * weighted).astype(jnp.bfloat16)
    by_sin = (column(xf_ref, HALF + j) * weighted).astype(jnp.bfloat16)
    rhs = jnp.concatenate([by_cos, by_sin], axis=1)
    re = jnp.dot(e_ref[:PLANE], rhs, preferred_element_type=jnp.float32)
    im = jnp.dot(e_ref[PLANE:], rhs, preferred_element_type=jnp.float32)
    rc, rs = re[:, :width], re[:, width:]
    ic, is_ = im[:, :width], im[:, width:]
    out_ref[0, 0, :, :width] = (rc - is_).astype(jnp.bfloat16)
    out_ref[0, 0, :, width:] = (-(ic + rs)).astype(jnp.bfloat16)
    out_ref[1, 0, :, :width] = (rc + is_).astype(jnp.bfloat16)
    out_ref[1, 0, :, width:] = (rs - ic).astype(jnp.bfloat16)


def analyse(e, xf, weighted):
    rows, width = weighted.shape
    out = pl.pallas_call(
        analyse_kernel,
        grid=(HALF,),
        out_shape=jax.ShapeDtypeStruct((2, HALF, PLANE, 2 * width), jnp.bfloat16),
        in_specs=[
            pl.BlockSpec((2 * PLANE, rows), lambda j: (0, 0)),
            pl.BlockSpec((rows, 2 * HALF), lambda j: (0, 0)),
            pl.BlockSpec((rows, width), lambda j: (0, 0)),
        ],
        out_specs=pl.BlockSpec((2, 1, PLANE, 2 * width), lambda j: (0, j, 0, 0)),
        compiler_params=pltpu.CompilerParams(vmem_limit_bytes=48 << 20),
    )(e, xf, weighted)
    return out.reshape(2 * HALF * PLANE, 2 * width)


def synthesize_kernel(et_ref, xf_ref, full_ref, out_ref):
    j = pl.program_id(0)
    width = out_ref.shape[1]
    pos = full_ref[0, 0].astype(jnp.float32)
    neg = full_ref[1, 0].astype(jnp.float32)
    pr, pi = pos[:, :width], pos[:, width:]
    nr, ni = neg[:, :width], neg[:, width:]
    top = jnp.concatenate([pr + nr, ni - pi], axis=1).astype(jnp.bfloat16)
    low = jnp.concatenate([-(pi + ni), nr - pr], axis=1).astype(jnp.bfloat16)
    field = jnp.dot(et_ref[:, :PLANE], top, preferred_element_type=jnp.float32)
    field = field + jnp.dot(et_ref[:, PLANE:], low, preferred_element_type=jnp.float32)
    add = column(xf_ref, j) * field[:, :width] + column(xf_ref, HALF + j) * field[:, width:]

    @pl.when(j == 0)
    def _():
        out_ref[...] = add

    @pl.when(j > 0)
    def _():
        out_ref[...] += add


def synthesize(et, xf, full):
    rows = et.shape[0]
    width = full.shape[1] // 2
    return pl.pallas_call(
        synthesize_kernel,
        grid=(HALF,),
        out_shape=jax.ShapeDtypeStruct((rows, width), jnp.float32),
        in_specs=[
            pl.BlockSpec((rows, 2 * PLANE), lambda j: (0, 0)),
            pl.BlockSpec((rows, 2 * HALF), lambda j: (0, 0)),
            pl.BlockSpec((2, 1, PLANE, 2 * width), lambda j: (0, j, 0, 0)),
        ],
        out_specs=pl.BlockSpec((rows, width), lambda j: (0, 0)),
        compiler_params=pltpu.CompilerParams(vmem_limit_bytes=48 << 20),
    )(et, xf, full.reshape(2, HALF, PLANE, 2 * width))


def filter_kernel(coef_ref, w_ref, out_ref):
    width = w_ref.shape[2]
    for m in range(w_ref.shape[0]):
        pair = coef_ref[m]
        by_re = jnp.dot(pair, w_ref[m, 0], preferred_element_type=jnp.float32)
        by_im = jnp.dot(pair, w_ref[m, 1], preferred_element_type=jnp.float32)
        out_ref[pl.ds(m, 1), :width] = by_re[0:1] - by_im[1:2]
        out_ref[pl.ds(m, 1), width:] = by_im[0:1] + by_re[1:2]


def filter_modes(coef, weight):
    modes, width = weight.shape[0], weight.shape[2]
    step = math.gcd(modes, 16)
    return pl.pallas_call(
        filter_kernel,
        grid=(modes // step,),
        out_shape=jax.ShapeDtypeStruct((modes, 2 * width), jnp.float32),
        in_specs=[
            pl.BlockSpec((step, 2, width), lambda m: (m, 0, 0)),
            pl.BlockSpec((step, 2, width, width), lambda m: (m, 0, 0, 0)),
        ],
        out_specs=pl.BlockSpec((step, 2 * width), lambda m: (m, 0)),
        compiler_params=pltpu.CompilerParams(vmem_limit_bytes=48 << 20),
    )(coef.reshape(modes, 2, width), weight)


def take_kernel(index_ref, src_ref, out_ref, wide, picked):
    @pl.when(pl.program_id(0) == 0)
    def _():
        wide[...] = src_ref[...].astype(jnp.float32)

    rows = out_ref.shape[0]
    base = pl.program_id(0) * rows
    unroll = math.gcd(rows, 16)

    def body(block, carry):
        at = block * unroll
        sources = [index_ref[base + at + k] for k in range(unroll)]
        found = [wide[pl.ds(source, 1), :] for source in sources]
        start = pl.multiple_of(at, unroll)
        picked[pl.ds(start, unroll), :] = jnp.concatenate(found, axis=0)
        return carry

    lax.fori_loop(0, rows // unroll, body, 0)
    out_ref[...] = picked[...].astype(out_ref.dtype)


def take_rows(table, index):
    n, width = table.shape
    m = index.shape[0]
    step = math.gcd(m, 512)
    return pl.pallas_call(
        take_kernel,
        out_shape=jax.ShapeDtypeStruct((m, width), table.dtype),
        grid_spec=pltpu.PrefetchScalarGridSpec(
            num_scalar_prefetch=1,
            grid=(m // step,),
            in_specs=[pl.BlockSpec((n, width), lambda b, index: (0, 0))],
            out_specs=pl.BlockSpec((step, width), lambda b, index: (b, 0)),
            scratch_shapes=[
                pltpu.VMEM((n, width), jnp.float32),
                pltpu.VMEM((step, width), jnp.float32),
            ],
        ),
        compiler_params=pltpu.CompilerParams(vmem_limit_bytes=48 << 20),
    )(index, table)


def grid_index(mode_table):
    kx = mode_table[0]
    slot = jnp.where(kx >= 0, kx, HALF - 1 - kx)
    return (slot * KY_COUNT + mode_table[1] - KY_LOW) * KZ_COUNT + mode_table[2] - KZ_LOW


def inverse_index(index):
    n = index.shape[0]
    lo = 128
    hi = n // lo
    ids = jnp.arange(n, dtype=jnp.int32)
    hot_lo = (index[:, None] % lo == jnp.arange(lo)[None, :]).astype(jnp.bfloat16)
    hit = index[None, :] // lo == jnp.arange(hi)[:, None]
    top = jnp.where(hit, ids[None, :] // lo, 0).astype(jnp.bfloat16)
    low = jnp.where(hit, ids[None, :] % lo, 0).astype(jnp.bfloat16)
    got = jnp.dot(jnp.concatenate([top, low], axis=0), hot_lo, preferred_element_type=jnp.float32)
    return (got[:hi] * lo + got[hi:]).astype(jnp.int32).reshape(n)


def on_device(features, coords, quad_weight, mode_table, mode_weight, lin_weight, bias):
    width = features.shape[1]
    n_groups = lax.axis_size("modes")
    group = lax.axis_index("modes")
    rows = features.shape[0] // n_groups
    features = lax.dynamic_slice_in_dim(features, group * rows, rows, 0)
    coords = lax.dynamic_slice_in_dim(coords, group * rows, rows, 1)
    quad = lax.dynamic_slice_in_dim(quad_weight, group * rows, rows, 0)
    own = mode_weight.shape[0]
    xf, parts = factors(coords)
    e, et = plane_factors(parts)
    index = grid_index(mode_table)
    inverse = inverse_index(index)
    weighted = (quad[:, None] * features.astype(jnp.float32)).astype(jnp.bfloat16)
    coef = analyse(e, xf, weighted)
    coef = take_rows(coef, index)
    core = lax.axis_index("core")
    halves = coef.reshape(-1, 2, n_groups, own, 2 * width)
    away = lax.dynamic_index_in_dim(halves, 1 - core, 1, False)
    home = lax.dynamic_index_in_dim(halves, core, 1, False)
    came = lax.ppermute(away, "core", [(0, 1), (1, 0)])
    both = (home.astype(jnp.float32) + came.astype(jnp.float32)).astype(jnp.bfloat16)
    coef = lax.all_to_all(both.reshape(-1, own, 2 * width), ("chip", "modes"), 0, 0)
    coef = jnp.sum(coef.astype(jnp.float32), axis=0).astype(jnp.bfloat16)
    filtered = filter_modes(coef, mode_weight).astype(jnp.bfloat16)
    share = jnp.sum(quad)
    high = lax.reduce_precision(share, 8, 7)
    mid = lax.reduce_precision(share - high, 8, 7)
    low = share - high - mid
    cells = jnp.pad(jnp.stack([high, mid, low]), (0, 2 * width - 3))
    cells = jnp.broadcast_to(cells[None], (TAIL, 2 * width)).astype(jnp.bfloat16)
    sent = jnp.concatenate([filtered, cells], axis=0)
    full = lax.all_gather(sent, AXES, axis=0, tiled=True)
    devices = full.shape[0] // (own + TAIL)
    shares = full.reshape(devices, own + TAIL, 2 * width)[:, own, :3]
    total = jnp.sum(shares.astype(jnp.float32))
    full = take_rows(full, inverse + inverse // own * TAIL)
    spectral = synthesize(et, xf, full)
    linear = jnp.dot(features, lin_weight, preferred_element_type=jnp.float32)
    pre = spectral / total + linear + bias[None, :]
    return jax.nn.gelu(pre, approximate=False).astype(jnp.bfloat16)


def solution(mesh):
    shape = (mesh.shape["pts"] // 2, 2, mesh.shape["modes"])
    mesh = Mesh(mesh.devices.reshape(shape), AXES)
    return jax.shard_map(
        on_device,
        mesh=mesh,
        in_specs=(
            P(PTS, None),
            P(None, PTS),
            P(PTS),
            P(),
            P(AXES, None, None, None),
            P(),
            P(),
        ),
        out_specs=P(AXES, None),
        check_vma=False,
    )
```

```python
import math

import jax
import jax.numpy as jnp
from jax import lax
from jax.experimental import pallas as pl
from jax.experimental.pallas import tpu as pltpu
from jax.sharding import Mesh
from jax.sharding import PartitionSpec as P

KX_LOW, KX_COUNT = -8, 16
KY_LOW, KY_COUNT = -8, 16
KZ_LOW, KZ_COUNT = 0, 32
HALF = KX_COUNT // 2
PLANE = KY_COUNT * KZ_COUNT
PTS = ("chip", "core")
AXES = PTS + ("modes",)
TAIL = 16


def cos_sin(turns):
    angle = (2.0 * math.pi) * (turns - jnp.round(turns))
    return jnp.cos(angle), jnp.sin(angle)


def factors(coords):
    x, y, z = coords[0], coords[1], coords[2]
    j = jnp.arange(HALF, dtype=jnp.float32) + 0.5
    xc, xs = cos_sin(j[:, None] * x[None, :])
    ky = jnp.arange(KY_COUNT, dtype=jnp.float32) + KY_LOW
    kz = jnp.arange(KZ_COUNT, dtype=jnp.float32) + KZ_LOW
    yc, ys = cos_sin(ky[:, None] * y[None, :])
    zc, zs = cos_sin(kz[:, None] * z[None, :] - 0.5 * x[None, :])
    return jnp.concatenate([xc, xs], axis=0).T, (yc, ys, zc, zs)


def plane_kernel(yc_ref, ys_ref, zc_ref, zs_ref, e_ref, et_ref):
    zc, zs = zc_ref[...], zs_ref[...]
    for k in range(KY_COUNT):
        yc, ys = yc_ref[pl.ds(k, 1)], ys_ref[pl.ds(k, 1)]
        re = yc * zc - ys * zs
        im = ys * zc + yc * zs
        e_ref[pl.ds(k * KZ_COUNT, KZ_COUNT)] = re.astype(jnp.bfloat16)
        e_ref[pl.ds(PLANE + k * KZ_COUNT, KZ_COUNT)] = im.astype(jnp.bfloat16)
    et_ref[...] = e_ref[...].T


def plane_factors(parts):
    rows = parts[0].shape[1]
    step = math.gcd(rows, 512)
    return pl.pallas_call(
        plane_kernel,
        grid=(rows // step,),
        out_shape=(
            jax.ShapeDtypeStruct((2 * PLANE, rows), jnp.bfloat16),
            jax.ShapeDtypeStruct((rows, 2 * PLANE), jnp.bfloat16),
        ),
        in_specs=[pl.BlockSpec((part.shape[0], step), lambda p: (0, p)) for part in parts],
        out_specs=(
            pl.BlockSpec((2 * PLANE, step), lambda p: (0, p)),
            pl.BlockSpec((step, 2 * PLANE), lambda p: (p, 0)),
        ),
        compiler_params=pltpu.CompilerParams(vmem_limit_bytes=48 << 20),
    )(*parts)


def column(table_ref, at):
    lanes = lax.broadcasted_iota(jnp.int32, table_ref.shape, 1)
    return jnp.sum(jnp.where(lanes == at, table_ref[...], 0.0), axis=1, keepdims=True)


def analyse_kernel(e_ref, xf_ref, weighted_ref, out_ref):
    j = pl.program_id(0)
    width = weighted_ref.shape[1]
    weighted = weighted_ref[...].astype(jnp.float32)
    by_cos = (column(xf_ref, j) * weighted).astype(jnp.bfloat16)
    by_sin = (column(xf_ref, HALF + j) * weighted).astype(jnp.bfloat16)
    rhs = jnp.concatenate([by_cos, by_sin], axis=1)
    re = jnp.dot(e_ref[:PLANE], rhs, preferred_element_type=jnp.float32)
    im = jnp.dot(e_ref[PLANE:], rhs, preferred_element_type=jnp.float32)
    rc, rs = re[:, :width], re[:, width:]
    ic, is_ = im[:, :width], im[:, width:]
    out_ref[0, 0, :, :width] = (rc - is_).astype(jnp.bfloat16)
    out_ref[0, 0, :, width:] = (-(ic + rs)).astype(jnp.bfloat16)
    out_ref[1, 0, :, :width] = (rc + is_).astype(jnp.bfloat16)
    out_ref[1, 0, :, width:] = (rs - ic).astype(jnp.bfloat16)


def analyse(e, xf, weighted):
    rows, width = weighted.shape
    out = pl.pallas_call(
        analyse_kernel,
        grid=(HALF,),
        out_shape=jax.ShapeDtypeStruct((2, HALF, PLANE, 2 * width), jnp.bfloat16),
        in_specs=[
            pl.BlockSpec((2 * PLANE, rows), lambda j: (0, 0)),
            pl.BlockSpec((rows, 2 * HALF), lambda j: (0, 0)),
            pl.BlockSpec((rows, width), lambda j: (0, 0)),
        ],
        out_specs=pl.BlockSpec((2, 1, PLANE, 2 * width), lambda j: (0, j, 0, 0)),
        compiler_params=pltpu.CompilerParams(vmem_limit_bytes=48 << 20),
    )(e, xf, weighted)
    return out.reshape(2 * HALF * PLANE, 2 * width)


def synthesize_kernel(et_ref, xf_ref, full_ref, out_ref):
    j = pl.program_id(0)
    width = out_ref.shape[1]
    pos = full_ref[0, 0].astype(jnp.float32)
    neg = full_ref[1, 0].astype(jnp.float32)
    pr, pi = pos[:, :width], pos[:, width:]
    nr, ni = neg[:, :width], neg[:, width:]
    top = jnp.concatenate([pr + nr, ni - pi], axis=1).astype(jnp.bfloat16)
    low = jnp.concatenate([-(pi + ni), nr - pr], axis=1).astype(jnp.bfloat16)
    field = jnp.dot(et_ref[:, :PLANE], top, preferred_element_type=jnp.float32)
    field = field + jnp.dot(et_ref[:, PLANE:], low, preferred_element_type=jnp.float32)
    add = column(xf_ref, j) * field[:, :width] + column(xf_ref, HALF + j) * field[:, width:]

    @pl.when(j == 0)
    def _():
        out_ref[...] = add

    @pl.when(j > 0)
    def _():
        out_ref[...] += add


def synthesize(et, xf, full):
    rows = et.shape[0]
    width = full.shape[1] // 2
    return pl.pallas_call(
        synthesize_kernel,
        grid=(HALF,),
        out_shape=jax.ShapeDtypeStruct((rows, width), jnp.float32),
        in_specs=[
            pl.BlockSpec((rows, 2 * PLANE), lambda j: (0, 0)),
            pl.BlockSpec((rows, 2 * HALF), lambda j: (0, 0)),
            pl.BlockSpec((2, 1, PLANE, 2 * width), lambda j: (0, j, 0, 0)),
        ],
        out_specs=pl.BlockSpec((rows, width), lambda j: (0, 0)),
        compiler_params=pltpu.CompilerParams(vmem_limit_bytes=48 << 20),
    )(et, xf, full.reshape(2, HALF, PLANE, 2 * width))


def filter_kernel(coef_ref, w_ref, out_ref):
    width = w_ref.shape[2]
    for m in range(w_ref.shape[0]):
        pair = coef_ref[m]
        by_re = jnp.dot(pair, w_ref[m, 0], preferred_element_type=jnp.float32)
        by_im = jnp.dot(pair, w_ref[m, 1], preferred_element_type=jnp.float32)
        out_ref[pl.ds(m, 1), :width] = by_re[0:1] - by_im[1:2]
        out_ref[pl.ds(m, 1), width:] = by_im[0:1] + by_re[1:2]


def filter_modes(coef, weight):
    modes, width = weight.shape[0], weight.shape[2]
    step = math.gcd(modes, 16)
    return pl.pallas_call(
        filter_kernel,
        grid=(modes // step,),
        out_shape=jax.ShapeDtypeStruct((modes, 2 * width), jnp.float32),
        in_specs=[
            pl.BlockSpec((step, 2, width), lambda m: (m, 0, 0)),
            pl.BlockSpec((step, 2, width, width), lambda m: (m, 0, 0, 0)),
        ],
        out_specs=pl.BlockSpec((step, 2 * width), lambda m: (m, 0)),
        compiler_params=pltpu.CompilerParams(vmem_limit_bytes=48 << 20),
    )(coef.reshape(modes, 2, width), weight)


def take_kernel(index_ref, *refs):
    *src_refs, out_ref, wide, picked = refs

    @pl.when(pl.program_id(0) == 0)
    def _():
        for i, src_ref in enumerate(src_refs):
            n = src_ref.shape[0]
            wide[i * n : (i + 1) * n] = src_ref[...].astype(jnp.float32)

    rows = out_ref.shape[0]
    base = pl.program_id(0) * rows
    unroll = math.gcd(rows, 16)

    def body(block, carry):
        at = block * unroll
        sources = [index_ref[base + at + k] for k in range(unroll)]
        found = [wide[pl.ds(source, 1), :] for source in sources]
        start = pl.multiple_of(at, unroll)
        picked[pl.ds(start, unroll), :] = jnp.concatenate(found, axis=0)
        return carry

    lax.fori_loop(0, rows // unroll, body, 0)
    out_ref[...] = picked[...].astype(out_ref.dtype)


def take_rows(tables, index):
    n, width = tables[0].shape
    m = index.shape[0]
    step = math.gcd(m, 512)
    return pl.pallas_call(
        take_kernel,
        out_shape=jax.ShapeDtypeStruct((m, width), tables[0].dtype),
        grid_spec=pltpu.PrefetchScalarGridSpec(
            num_scalar_prefetch=1,
            grid=(m // step,),
            in_specs=[pl.BlockSpec((n, width), lambda b, index: (0, 0)) for _ in tables],
            out_specs=pl.BlockSpec((step, width), lambda b, index: (b, 0)),
            scratch_shapes=[
                pltpu.VMEM((len(tables) * n, width), jnp.float32),
                pltpu.VMEM((step, width), jnp.float32),
            ],
        ),
        compiler_params=pltpu.CompilerParams(vmem_limit_bytes=48 << 20),
    )(index, *tables)


def grid_index(mode_table):
    kx = mode_table[0]
    slot = jnp.where(kx >= 0, kx, HALF - 1 - kx)
    return (slot * KY_COUNT + mode_table[1] - KY_LOW) * KZ_COUNT + mode_table[2] - KZ_LOW


def inverse_index(index):
    n = index.shape[0]
    lo = 128
    hi = n // lo
    ids = jnp.arange(n, dtype=jnp.int32)
    hot_lo = (index[:, None] % lo == jnp.arange(lo)[None, :]).astype(jnp.bfloat16)
    hit = index[None, :] // lo == jnp.arange(hi)[:, None]
    top = jnp.where(hit, ids[None, :] // lo, 0).astype(jnp.bfloat16)
    low = jnp.where(hit, ids[None, :] % lo, 0).astype(jnp.bfloat16)
    got = jnp.dot(jnp.concatenate([top, low], axis=0), hot_lo, preferred_element_type=jnp.float32)
    return (got[:hi] * lo + got[hi:]).astype(jnp.int32).reshape(n)


def on_device(features, coords, quad_weight, mode_table, mode_weight, lin_weight, bias):
    width = features.shape[1]
    n_groups = lax.axis_size("modes")
    group = lax.axis_index("modes")
    rows = features.shape[0] // n_groups
    features = lax.dynamic_slice_in_dim(features, group * rows, rows, 0)
    coords = lax.dynamic_slice_in_dim(coords, group * rows, rows, 1)
    quad = lax.dynamic_slice_in_dim(quad_weight, group * rows, rows, 0)
    own = mode_weight.shape[0]
    xf, parts = factors(coords)
    e, et = plane_factors(parts)
    index = grid_index(mode_table)
    inverse = inverse_index(index)
    weighted = (quad[:, None] * features.astype(jnp.float32)).astype(jnp.bfloat16)
    coef = analyse(e, xf, weighted)
    coef = take_rows([coef], index)
    core = lax.axis_index("core")
    halves = coef.reshape(-1, 2, n_groups, own, 2 * width)
    away = lax.dynamic_index_in_dim(halves, 1 - core, 1, False)
    home = lax.dynamic_index_in_dim(halves, core, 1, False)
    came = lax.ppermute(away, "core", [(0, 1), (1, 0)])
    both = (home.astype(jnp.float32) + came.astype(jnp.float32)).astype(jnp.bfloat16)
    coef = lax.all_to_all(both.reshape(-1, own, 2 * width), ("chip", "modes"), 0, 0)
    coef = jnp.sum(coef.astype(jnp.float32), axis=0).astype(jnp.bfloat16)
    filtered = filter_modes(coef, mode_weight).astype(jnp.bfloat16)
    share = jnp.sum(quad)
    high = lax.reduce_precision(share, 8, 7)
    mid = lax.reduce_precision(share - high, 8, 7)
    low = share - high - mid
    cells = jnp.pad(jnp.stack([high, mid, low]), (0, 2 * width - 3))
    cells = jnp.broadcast_to(cells[None], (TAIL, 2 * width)).astype(jnp.bfloat16)
    sent = jnp.concatenate([filtered, cells], axis=0)
    sends = lax.axis_size("chip") * n_groups
    block = own + TAIL
    copies = jnp.broadcast_to(sent[None], (sends, block, 2 * width))
    mine = lax.all_to_all(copies, ("chip", "modes"), 0, 0)
    other = lax.ppermute(mine, "core", [(0, 1), (1, 0)])
    shares = mine[:, own, :3].astype(jnp.float32) + other[:, own, :3].astype(jnp.float32)
    total = jnp.sum(shares)
    device = inverse // own
    pair = device // n_groups
    side = jnp.where(pair % 2 == core, 0, sends)
    place = side + pair // 2 * n_groups + device % n_groups
    tables = [t.reshape(sends * block, 2 * width) for t in (mine, other)]
    full = take_rows(tables, place * block + inverse % own)
    spectral = synthesize(et, xf, full)
    linear = jnp.dot(features, lin_weight, preferred_element_type=jnp.float32)
    pre = spectral / total + linear + bias[None, :]
    return jax.nn.gelu(pre, approximate=False).astype(jnp.bfloat16)


def solution(mesh):
    shape = (mesh.shape["pts"] // 2, 2, mesh.shape["modes"])
    mesh = Mesh(mesh.devices.reshape(shape), AXES)
    return jax.shard_map(
        on_device,
        mesh=mesh,
        in_specs=(
            P(PTS, None),
            P(None, PTS),
            P(PTS),
            P(),
            P(AXES, None, None, None),
            P(),
            P(),
        ),
        out_specs=P(AXES, None),
        check_vma=False,
    )
```

```python
import math

import jax
import jax.numpy as jnp
from jax import lax
from jax.experimental import pallas as pl
from jax.experimental.pallas import tpu as pltpu
from jax.sharding import Mesh
from jax.sharding import PartitionSpec as P

KX_LOW, KX_COUNT = -8, 16
KY_LOW, KY_COUNT = -8, 16
KZ_LOW, KZ_COUNT = 0, 32
HALF = KX_COUNT // 2
PLANE = KY_COUNT * KZ_COUNT
PTS = ("chip", "core")
AXES = PTS + ("modes",)
TAIL = 16


def cos_sin(turns):
    angle = (2.0 * math.pi) * (turns - jnp.round(turns))
    return jnp.cos(angle), jnp.sin(angle)


def factors(coords):
    x, y, z = coords[0], coords[1], coords[2]
    j = jnp.arange(HALF, dtype=jnp.float32) + 0.5
    xc, xs = cos_sin(j[:, None] * x[None, :])
    ky = jnp.arange(KY_COUNT, dtype=jnp.float32) + KY_LOW
    kz = jnp.arange(KZ_COUNT, dtype=jnp.float32) + KZ_LOW
    yc, ys = cos_sin(ky[:, None] * y[None, :])
    zc, zs = cos_sin(kz[:, None] * z[None, :] - 0.5 * x[None, :])
    return jnp.concatenate([xc, xs], axis=0).T, (yc, ys, zc, zs)


def plane_kernel(yc_ref, ys_ref, zc_ref, zs_ref, e_ref, et_ref):
    zc, zs = zc_ref[...], zs_ref[...]
    for k in range(KY_COUNT):
        yc, ys = yc_ref[pl.ds(k, 1)], ys_ref[pl.ds(k, 1)]
        re = yc * zc - ys * zs
        im = ys * zc + yc * zs
        e_ref[pl.ds(k * KZ_COUNT, KZ_COUNT)] = re.astype(jnp.bfloat16)
        e_ref[pl.ds(PLANE + k * KZ_COUNT, KZ_COUNT)] = im.astype(jnp.bfloat16)
    et_ref[...] = e_ref[...].T


def plane_factors(parts):
    rows = parts[0].shape[1]
    step = math.gcd(rows, 512)
    return pl.pallas_call(
        plane_kernel,
        grid=(rows // step,),
        out_shape=(
            jax.ShapeDtypeStruct((2 * PLANE, rows), jnp.bfloat16),
            jax.ShapeDtypeStruct((rows, 2 * PLANE), jnp.bfloat16),
        ),
        in_specs=[pl.BlockSpec((part.shape[0], step), lambda p: (0, p)) for part in parts],
        out_specs=(
            pl.BlockSpec((2 * PLANE, step), lambda p: (0, p)),
            pl.BlockSpec((step, 2 * PLANE), lambda p: (p, 0)),
        ),
        compiler_params=pltpu.CompilerParams(vmem_limit_bytes=48 << 20),
    )(*parts)


def column(table_ref, at):
    lanes = lax.broadcasted_iota(jnp.int32, table_ref.shape, 1)
    return jnp.sum(jnp.where(lanes == at, table_ref[...], 0.0), axis=1, keepdims=True)


def analyse_kernel(e_ref, xf_ref, weighted_ref, out_ref):
    j = pl.program_id(0)
    width = weighted_ref.shape[1]
    weighted = weighted_ref[...].astype(jnp.float32)
    by_cos = (column(xf_ref, j) * weighted).astype(jnp.bfloat16)
    by_sin = (column(xf_ref, HALF + j) * weighted).astype(jnp.bfloat16)
    rhs = jnp.concatenate([by_cos, by_sin], axis=1)
    re = jnp.dot(e_ref[:PLANE], rhs, preferred_element_type=jnp.float32)
    im = jnp.dot(e_ref[PLANE:], rhs, preferred_element_type=jnp.float32)
    rc, rs = re[:, :width], re[:, width:]
    ic, is_ = im[:, :width], im[:, width:]
    out_ref[0, 0, :, :width] = (rc - is_).astype(jnp.bfloat16)
    out_ref[0, 0, :, width:] = (-(ic + rs)).astype(jnp.bfloat16)
    out_ref[1, 0, :, :width] = (rc + is_).astype(jnp.bfloat16)
    out_ref[1, 0, :, width:] = (rs - ic).astype(jnp.bfloat16)


def analyse(e, xf, weighted):
    rows, width = weighted.shape
    out = pl.pallas_call(
        analyse_kernel,
        grid=(HALF,),
        out_shape=jax.ShapeDtypeStruct((2, HALF, PLANE, 2 * width), jnp.bfloat16),
        in_specs=[
            pl.BlockSpec((2 * PLANE, rows), lambda j: (0, 0)),
            pl.BlockSpec((rows, 2 * HALF), lambda j: (0, 0)),
            pl.BlockSpec((rows, width), lambda j: (0, 0)),
        ],
        out_specs=pl.BlockSpec((2, 1, PLANE, 2 * width), lambda j: (0, j, 0, 0)),
        compiler_params=pltpu.CompilerParams(vmem_limit_bytes=48 << 20),
    )(e, xf, weighted)
    return out.reshape(2 * HALF * PLANE, 2 * width)


def synthesize_kernel(et_ref, xf_ref, full_ref, out_ref):
    j = pl.program_id(0)
    width = out_ref.shape[1]
    pos = full_ref[0, 0].astype(jnp.float32)
    neg = full_ref[1, 0].astype(jnp.float32)
    pr, pi = pos[:, :width], pos[:, width:]
    nr, ni = neg[:, :width], neg[:, width:]
    top = jnp.concatenate([pr + nr, ni - pi], axis=1).astype(jnp.bfloat16)
    low = jnp.concatenate([-(pi + ni), nr - pr], axis=1).astype(jnp.bfloat16)
    field = jnp.dot(et_ref[:, :PLANE], top, preferred_element_type=jnp.float32)
    field = field + jnp.dot(et_ref[:, PLANE:], low, preferred_element_type=jnp.float32)
    add = column(xf_ref, j) * field[:, :width] + column(xf_ref, HALF + j) * field[:, width:]

    @pl.when(j == 0)
    def _():
        out_ref[...] = add

    @pl.when(j > 0)
    def _():
        out_ref[...] += add


def synthesize(et, xf, full):
    rows = et.shape[0]
    width = full.shape[1] // 2
    return pl.pallas_call(
        synthesize_kernel,
        grid=(HALF,),
        out_shape=jax.ShapeDtypeStruct((rows, width), jnp.float32),
        in_specs=[
            pl.BlockSpec((rows, 2 * PLANE), lambda j: (0, 0)),
            pl.BlockSpec((rows, 2 * HALF), lambda j: (0, 0)),
            pl.BlockSpec((2, 1, PLANE, 2 * width), lambda j: (0, j, 0, 0)),
        ],
        out_specs=pl.BlockSpec((rows, width), lambda j: (0, 0)),
        compiler_params=pltpu.CompilerParams(vmem_limit_bytes=48 << 20),
    )(et, xf, full.reshape(2, HALF, PLANE, 2 * width))


def filter_kernel(coef_ref, w_ref, out_ref):
    width = w_ref.shape[2]
    for m in range(w_ref.shape[0]):
        pair = coef_ref[m]
        by_re = jnp.dot(pair, w_ref[m, 0], preferred_element_type=jnp.float32)
        by_im = jnp.dot(pair, w_ref[m, 1], preferred_element_type=jnp.float32)
        out_ref[pl.ds(m, 1), :width] = by_re[0:1] - by_im[1:2]
        out_ref[pl.ds(m, 1), width:] = by_im[0:1] + by_re[1:2]


def filter_modes(coef, weight):
    modes, width = weight.shape[0], weight.shape[2]
    step = math.gcd(modes, 32)
    return pl.pallas_call(
        filter_kernel,
        grid=(modes // step,),
        out_shape=jax.ShapeDtypeStruct((modes, 2 * width), jnp.float32),
        in_specs=[
            pl.BlockSpec((step, 2, width), lambda m: (m, 0, 0)),
            pl.BlockSpec((step, 2, width, width), lambda m: (m, 0, 0, 0)),
        ],
        out_specs=pl.BlockSpec((step, 2 * width), lambda m: (m, 0)),
        compiler_params=pltpu.CompilerParams(vmem_limit_bytes=48 << 20),
    )(coef.reshape(modes, 2, width), weight)


def take_kernel(index_ref, *refs):
    *src_refs, out_ref, wide, picked = refs

    @pl.when(pl.program_id(0) == 0)
    def _():
        for i, src_ref in enumerate(src_refs):
            n = src_ref.shape[0]
            wide[i * n : (i + 1) * n] = src_ref[...].astype(jnp.float32)

    rows = out_ref.shape[0]
    base = pl.program_id(0) * rows
    unroll = math.gcd(rows, 32)

    def body(block, carry):
        at = block * unroll
        sources = [index_ref[base + at + k] for k in range(unroll)]
        found = [wide[pl.ds(source, 1), :] for source in sources]
        start = pl.multiple_of(at, unroll)
        picked[pl.ds(start, unroll), :] = jnp.concatenate(found, axis=0)
        return carry

    lax.fori_loop(0, rows // unroll, body, 0)
    out_ref[...] = picked[...].astype(out_ref.dtype)


def take_rows(tables, index):
    n, width = tables[0].shape
    m = index.shape[0]
    step = math.gcd(m, 512)
    return pl.pallas_call(
        take_kernel,
        out_shape=jax.ShapeDtypeStruct((m, width), tables[0].dtype),
        grid_spec=pltpu.PrefetchScalarGridSpec(
            num_scalar_prefetch=1,
            grid=(m // step,),
            in_specs=[pl.BlockSpec((n, width), lambda b, index: (0, 0)) for _ in tables],
            out_specs=pl.BlockSpec((step, width), lambda b, index: (b, 0)),
            scratch_shapes=[
                pltpu.VMEM((len(tables) * n, width), jnp.float32),
                pltpu.VMEM((step, width), jnp.float32),
            ],
        ),
        compiler_params=pltpu.CompilerParams(vmem_limit_bytes=48 << 20),
    )(index, *tables)


def grid_index(mode_table):
    kx = mode_table[0]
    slot = jnp.where(kx >= 0, kx, HALF - 1 - kx)
    return (slot * KY_COUNT + mode_table[1] - KY_LOW) * KZ_COUNT + mode_table[2] - KZ_LOW


def inverse_index(index):
    n = index.shape[0]
    lo = 128
    hi = n // lo
    ids = jnp.arange(n, dtype=jnp.int32)
    hot_lo = (index[:, None] % lo == jnp.arange(lo)[None, :]).astype(jnp.bfloat16)
    hit = index[None, :] // lo == jnp.arange(hi)[:, None]
    top = jnp.where(hit, ids[None, :] // lo, 0).astype(jnp.bfloat16)
    low = jnp.where(hit, ids[None, :] % lo, 0).astype(jnp.bfloat16)
    got = jnp.dot(jnp.concatenate([top, low], axis=0), hot_lo, preferred_element_type=jnp.float32)
    return (got[:hi] * lo + got[hi:]).astype(jnp.int32).reshape(n)


def on_device(features, coords, quad_weight, mode_table, mode_weight, lin_weight, bias):
    width = features.shape[1]
    n_groups = lax.axis_size("modes")
    group = lax.axis_index("modes")
    rows = features.shape[0] // n_groups
    features = lax.dynamic_slice_in_dim(features, group * rows, rows, 0)
    coords = lax.dynamic_slice_in_dim(coords, group * rows, rows, 1)
    quad = lax.dynamic_slice_in_dim(quad_weight, group * rows, rows, 0)
    own = mode_weight.shape[0]
    xf, parts = factors(coords)
    e, et = plane_factors(parts)
    index = grid_index(mode_table)
    inverse = inverse_index(index)
    weighted = (quad[:, None] * features.astype(jnp.float32)).astype(jnp.bfloat16)
    coef = analyse(e, xf, weighted)
    coef = take_rows([coef], index)
    core = lax.axis_index("core")
    halves = coef.reshape(-1, 2, n_groups, own, 2 * width)
    away = lax.dynamic_index_in_dim(halves, 1 - core, 1, False)
    home = lax.dynamic_index_in_dim(halves, core, 1, False)
    came = lax.ppermute(away, "core", [(0, 1), (1, 0)])
    both = (home.astype(jnp.float32) + came.astype(jnp.float32)).astype(jnp.bfloat16)
    coef = lax.all_to_all(both.reshape(-1, own, 2 * width), ("chip", "modes"), 0, 0)
    coef = jnp.sum(coef.astype(jnp.float32), axis=0).astype(jnp.bfloat16)
    filtered = filter_modes(coef, mode_weight).astype(jnp.bfloat16)
    share = jnp.sum(quad)
    high = lax.reduce_precision(share, 8, 7)
    mid = lax.reduce_precision(share - high, 8, 7)
    low = share - high - mid
    cells = jnp.pad(jnp.stack([high, mid, low]), (0, 2 * width - 3))
    cells = jnp.broadcast_to(cells[None], (TAIL, 2 * width)).astype(jnp.bfloat16)
    sent = jnp.concatenate([filtered, cells], axis=0)
    sends = lax.axis_size("chip") * n_groups
    block = own + TAIL
    copies = jnp.broadcast_to(sent[None], (sends, block, 2 * width))
    mine = lax.all_to_all(copies, ("chip", "modes"), 0, 0)
    other = lax.ppermute(mine, "core", [(0, 1), (1, 0)])
    shares = mine[:, own, :3].astype(jnp.float32) + other[:, own, :3].astype(jnp.float32)
    total = jnp.sum(shares)
    device = inverse // own
    pair = device // n_groups
    side = jnp.where(pair % 2 == core, 0, sends)
    place = side + pair // 2 * n_groups + device % n_groups
    tables = [t.reshape(sends * block, 2 * width) for t in (mine, other)]
    full = take_rows(tables, place * block + inverse % own)
    spectral = synthesize(et, xf, full)
    linear = jnp.dot(features, lin_weight, preferred_element_type=jnp.float32)
    pre = spectral / total + linear + bias[None, :]
    return jax.nn.gelu(pre, approximate=False).astype(jnp.bfloat16)


def solution(mesh):
    shape = (mesh.shape["pts"] // 2, 2, mesh.shape["modes"])
    mesh = Mesh(mesh.devices.reshape(shape), AXES)
    return jax.shard_map(
        on_device,
        mesh=mesh,
        in_specs=(
            P(PTS, None),
            P(None, PTS),
            P(PTS),
            P(),
            P(AXES, None, None, None),
            P(),
            P(),
        ),
        out_specs=P(AXES, None),
        check_vma=False,
    )
```
